128 devices in a mesh: dom: 16 (over z, y_hi, core), repl: 8 (over y_lo, x).
Axes of the slice: x: 4, y: 4 (y_hi: 2, y_lo: 2; y = y_hi * 2 + y_lo), z: 4, core: 2. Of those that a mesh axis runs over, the one named last changes fastest.
Arguments:
- features: bfloat16 [32768, 512], P(('dom', 'repl')), may hold values from -6 to 6
- cotangent: bfloat16 [32768, 512], P(('dom', 'repl')), may hold values from -6 to 6
- weight: bfloat16 [512, 512], replicated, may hold values from -0.25 to 0.25
- tiles: bfloat16 [16, 8, 16, 16, 128, 128], P('dom', 'repl'), may hold values from -0.0625 to 0.0625
- tile_rows: int32 [16, 8, 16, 16], P('dom', 'repl'), may hold values from 0 to 15
- tile_cols: int32 [16, 8, 16, 16], P('dom', 'repl'), may hold values from 0 to 1
- tile_counts: int32 [16, 8, 16], P('dom', 'repl'), may hold values from 1 to 16, as said below
Outputs:
- activated: bfloat16 [32768, 512], P(('dom', 'repl'))
- feature_grad: bfloat16 [32768, 512], P(('dom', 'repl'))
- weight_grad: float32 [512, 512], replicated
The draws below stay inside these ranges and needn't reach their ends.
Inputs may be any that keep to these rules, and one draw needn't show every extreme that they name: `tile_counts`: live tiles of each row block, column group and column block; some entry equals 16 in every draw.
All inputs are finite; a program needn't handle non-finite values.
Results may differ from the reference program's by a relative error of at most 0.006.
Values may be sent and summed in bfloat16 or wider, within the bound.
A program may use at most 64 MiB of HBM per device.

```python
import jax
import jax.numpy as jnp
from jax import lax

F = 512
TILE = 128
ROWS_DEV = 256
MAXT = 16
BLOCKS = 16
SUBS = 8
COLTILES = 2
ROWTILES = 16
VERTS = 32768


def draw_tile_counts(key, part):
    keys = jax.random.split(jax.random.fold_in(key, 17), 5)
    base = jax.random.randint(keys[0], (BLOCKS, SUBS, BLOCKS), 1, MAXT + 1)
    heavy = jax.random.randint(keys[1], (BLOCKS, 1, 1), 0, 4) == 0
    counts = jnp.where(heavy, MAXT, base)
    first = jax.random.randint(keys[2], (), 0, BLOCKS)
    second = jax.random.randint(keys[3], (), 0, SUBS)
    third = jax.random.randint(keys[4], (), 0, BLOCKS)
    counts = counts.at[first, second, third].set(MAXT)
    return counts.astype(jnp.int32)


def touch_ends(result, own_key, smallest, largest):
    longest = result.shape.index(max(result.shape))
    spots = []
    for shift in (0, 1):
        where = [jax.random.randint(jax.random.fold_in(own_key, axis), (), 0, length) for axis, length in enumerate(result.shape)]
        where[longest] = (where[longest] + shift) % result.shape[longest]
        spots.append(tuple(where))
    return result.at[spots[0]].set(smallest).at[spots[1]].set(largest)


def levels(key, dims, cuts, smallest, top_value):
    level = 1.0
    for position, parts in cuts:
        heights = jax.random.uniform(jax.random.fold_in(jax.random.fold_in(key, 6), position), (parts,), jnp.float32, smallest / len(cuts), top_value / len(cuts))
        level = level * jnp.repeat(jnp.exp(heights), dims[position] // parts).reshape((-1,) + (1,) * (len(dims) - 1 - position))
    return level


def scatter_about(stream_key, dims, scale, most, shards=(), held_as=jnp.bfloat16):
    entries = scale * jax.random.normal(stream_key, dims, jnp.float32)
    if shards:
        entries = entries * levels(stream_key, dims, shards, -0.22, 0.18)
    return jnp.clip(entries, -most, most).astype(held_as)


def setup_inputs(seed: int = 0) -> dict:
    streams_of = jax.random.split(jax.random.key(seed), 8)
    return {
        "features": scatter_about(streams_of[0], (VERTS, F), 1.0, 6.0, ((0, 128),)),
        "cotangent": scatter_about(streams_of[1], (VERTS, F), 1.0, 6.0, ((0, 128),)),
        "weight": scatter_about(streams_of[2], (F, F), F ** -0.5, 0.25),
        "tiles": scatter_about(streams_of[3], (BLOCKS, SUBS, BLOCKS, MAXT, TILE, TILE), (BLOCKS * MAXT * TILE * TILE // (2 * ROWS_DEV)) ** -0.5, 0.0625, ((0, 16), (1, 8))),
        "tile_rows": touch_ends(jax.random.randint(streams_of[4], (BLOCKS, SUBS, BLOCKS, MAXT), 0, ROWTILES), jax.random.fold_in(streams_of[4], 1), 0, ROWTILES - 1).astype(jnp.int32),
        "tile_cols": touch_ends(jax.random.randint(streams_of[5], (BLOCKS, SUBS, BLOCKS, MAXT), 0, COLTILES), jax.random.fold_in(streams_of[5], 1), 0, COLTILES - 1).astype(jnp.int32),
        "tile_counts": draw_tile_counts(jax.random.fold_in(streams_of[7], 71), 0),
    }


def silu_slope(preact):
    sig = jax.nn.sigmoid(preact)
    return sig * (1.0 + preact * (1.0 - sig))


def reference(features, cotangent, weight, tiles, tile_rows, tile_cols, tile_counts):
    nblk = BLOCKS
    ngrp = SUBS
    owners = features.reshape(nblk * ngrp, COLTILES, TILE, F)

    def live_slab(row_block, member, column):
        slab = tiles[row_block, member, column].astype(jnp.float32)
        alive = (jnp.arange(MAXT) < tile_counts[row_block, member, column]).astype(jnp.float32)
        return slab * alive[:, None, None]

    def forward_block(row_block):
        def visit(totals, pair):
            member = pair // nblk
            column = pair % nblk
            slab = live_slab(row_block, member, column)
            source = owners[column * ngrp + member]
            picked = source[tile_cols[row_block, member, column]].astype(jnp.float32)
            prod = jnp.einsum("tab,tbf->taf", slab, picked)
            return totals.at[tile_rows[row_block, member, column]].add(prod), None

        start = jnp.zeros((ROWTILES, TILE, F), jnp.float32)
        totals, _ = lax.scan(visit, start, jnp.arange(nblk * ngrp))
        return totals.reshape(ngrp * ROWS_DEV, F)

    aggregated = lax.map(forward_block, jnp.arange(nblk)).reshape(VERTS, F)
    agg_rounded = aggregated.astype(jnp.bfloat16)
    preact = jnp.dot(agg_rounded, weight, preferred_element_type=jnp.float32)
    activated = jax.nn.silu(preact).astype(jnp.bfloat16)
    pre_grad = (cotangent.astype(jnp.float32) * silu_slope(preact)).astype(jnp.bfloat16)
    weight_grad = jnp.dot(agg_rounded.T, pre_grad, preferred_element_type=jnp.float32) * (float(VERTS) ** -0.5)
    agg_grad = jnp.dot(pre_grad, weight.T, preferred_element_type=jnp.float32).astype(jnp.bfloat16)
    grad_tiles = agg_grad.reshape(nblk, ROWTILES, TILE, F)

    def backward_owner(owner):
        column = owner // ngrp
        member = owner % ngrp

        def visit(totals, row_block):
            slab = live_slab(row_block, member, column)
            picked = grad_tiles[row_block][tile_rows[row_block, member, column]].astype(jnp.float32)
            prod = jnp.einsum("tab,taf->tbf", slab, picked)
            return totals.at[tile_cols[row_block, member, column]].add(prod), None

        start = jnp.zeros((COLTILES, TILE, F), jnp.float32)
        totals, _ = lax.scan(visit, start, jnp.arange(nblk))
        return totals.reshape(ROWS_DEV, F)

    feature_grad = lax.map(backward_owner, jnp.arange(nblk * ngrp)).reshape(VERTS, F).astype(jnp.bfloat16)
    return (activated, feature_grad, weight_grad)
```

```python
import functools

import jax
import jax.numpy as jnp
from jax import lax
from jax.experimental import pallas as pl
from jax.experimental.pallas import tpu as pltpu
from jax.sharding import PartitionSpec as P

F32 = jnp.float32
BF16 = jnp.bfloat16
MESH = pl.DeviceIdType.MESH
Z, YH, CO, YL, X = 4, 2, 2, 2, 4
NDOM, NREP = Z * YH * CO, YL * X


class Names:
    def __init__(self):
        self.count = 0

    def take(self, n=1):
        base = self.count
        self.count += n
        return base


def message_table():
    names = Names()
    table = {}
    for h in (0, 1):
        for kind, n in (("zp", 2), ("zm", 2), ("y", 1), ("f", 2), ("sib", 8)):
            table["A", kind, h] = names.take(n)
        for kind, n in (("2p", 1), ("2m", 1), ("p", 1), ("m", 1), ("y", 1)):
            table["B", kind, h] = names.take(n)
        for kind, n in (("xp", 2), ("xm", 2), ("y", 1), ("f", 2)):
            table["D", kind, h] = names.take(n)
        for kind, n in (("sib", 8), ("2p", 1), ("2m", 1), ("p", 2), ("m", 2), ("y", 1)):
            table["E", kind, h] = names.take(n)
    for kind in ("rc", "gc"):
        table["W", kind] = names.take(1)
    for kind in ("rz", "ry", "rx", "gx", "gy", "gz"):
        table["W", kind] = names.take(3)
    return table, names.count


def kernel(dims, table, chain_ref, feat_ref, cot_ref, w_ref, tiles_ref,
           act_ref, fgrad_ref, wgrad_ref, *scratch):
    rows, width, tile, slots = dims
    half = width // 2
    scale = float(rows * NDOM * NREP) ** (-0.5)
    (tbuf, rbuf, adj, fbuf, gbuf, pacc, eacc, agg, preact,
     bs2, bsp, bsm, bsy, br2p, br2m, brp, brm, bry,
     ess, es2, esp, esm, esy, ers, er2p, er2m, erp, erm, ery,
     wpart, wrc, wzb, wrz, w2, wry, w3, wrx, wfull,
     tsem, fsem, ssem, rsem) = scratch

    dom = lax.axis_index("dom")
    rep = lax.axis_index("repl")
    co = lax.rem(dom, 2)
    yh = lax.rem(lax.div(dom, 2), 2)
    z = lax.div(dom, 4)
    x = lax.rem(rep, 4)
    yl = lax.div(rep, 4)
    y = yh * 2 + yl

    def turn(v, by):
        return lax.rem(v + by, 4)

    zu, zd, z2 = turn(z, 1), turn(z, 3), turn(z, 2)
    xu, xd, x2 = turn(x, 1), turn(x, 3), turn(x, 2)

    def did(z_, yh_, co_):
        return z_ * 4 + yh_ * 2 + co_

    def at_y(y_):
        return (did(z, lax.div(y_, 2), co), lax.rem(y_, 2) * 4 + x)

    dev_sib = (did(z, yh, 1 - co), rep)
    dev_zu, dev_zd = (did(zu, yh, co), rep), (did(zd, yh, co), rep)
    dev_yp = (did(z, 1 - yh, co), rep)
    dev_xu, dev_xd = (dom, yl * 4 + xu), (dom, yl * 4 + xd)
    dev_yl = (dom, (1 - yl) * 4 + x)
    zpeers = [(did(turn(z, k), yh, co), rep) for k in (1, 2, 3)]
    ypeers = [at_y(turn(y, k)) for k in (1, 2, 3)]
    xpeers = [(dom, yl * 4 + turn(x, k)) for k in (1, 2, 3)]

    pending = []

    def send(src, dst, number, dev, slot=None):
        arrival = number if slot is None else number + slot
        copy = pltpu.make_async_remote_copy(
            src_ref=src, dst_ref=dst, send_sem=ssem.at[len(pending)], recv_sem=rsem.at[arrival],
            device_id=dev, device_id_type=MESH)
        copy.start()
        pending.append(copy)

    def arrived(dst, number):
        pltpu.make_async_remote_copy(
            src_ref=dst, dst_ref=dst, send_sem=ssem.at[0], recv_sem=rsem.at[number],
            device_id=dev_sib, device_id_type=MESH).wait_recv()

    def slab(c):
        return pl.ds(pl.multiple_of(c * rows, rows), rows)

    for c in range(NDOM):
        pltpu.make_async_copy(tiles_ref.at[c], tbuf.at[c], tsem.at[c]).start()
    for h in (0, 1):
        pltpu.make_async_copy(
            feat_ref.at[:, h * half:(h + 1) * half], fbuf.at[h, slab(dom)], fsem.at[h]).start()
    barrier = pltpu.get_barrier_semaphore()
    partners = [dev_sib] + zpeers + ypeers + xpeers
    for dev in partners:
        pl.semaphore_signal(barrier, inc=1, device_id=dev, device_id_type=MESH)
    rbuf[slots] = jnp.zeros((tile, tile), F32)
    pl.semaphore_wait(barrier, len(partners))

    def a_slot(kind, core):
        return {
            "own": did(z, yh, core), "par": did(z, 1 - yh, core),
            "zp0": did(zd, 0, core), "zp1": did(zd, 1, core),
            "zm0": did(zu, 0, core), "zm1": did(zu, 1, core),
            "f0": did(z2, 0, core), "f1": did(z2, 1, core),
        }[kind]

    a_kinds = ("own", "par", "zp0", "zm1", "zp1", "zm0", "f0", "f1")

    def a_send(h, kind, number, dev, slot=None):
        block = fbuf.at[h, slab(a_slot(kind, co))]
        send(block, block, number, dev, slot)

    def a_sib(h, kind):
        a_send(h, kind, table["A", "sib", h] + a_kinds.index(kind), dev_sib)

    def a_wait(h, kind, number):
        arrived(fbuf.at[h, slab(a_slot(kind, co))], number)

    def a_own(h):
        pltpu.make_async_copy(
            feat_ref.at[:, h * half:(h + 1) * half], fbuf.at[h, slab(dom)], fsem.at[h]).wait()
        a_send(h, "own", table["A", "zp", h], dev_zu, yh)
        a_send(h, "own", table["A", "zm", h], dev_zd, yh)
        a_send(h, "own", table["A", "y", h], dev_yp)
        a_sib(h, "own")

    def a_par(h):
        a_wait(h, "par", table["A", "y", h])
        a_send(h, "par", table["A", "zp", h], dev_zu, 1 - yh)
        a_send(h, "par", table["A", "zm", h], dev_zd, 1 - yh)
        a_sib(h, "par")

    def a_ring(h):
        a_wait(h, "zp0", table["A", "zp", h])
        a_send(h, "zp0", table["A", "f", h], dev_zu)
        a_sib(h, "zp0")
        a_wait(h, "zm1", table["A", "zm", h] + 1)
        a_send(h, "zm1", table["A", "f", h] + 1, dev_zd)
        a_sib(h, "zm1")
        a_wait(h, "zp1", table["A", "zp", h] + 1)
        a_sib(h, "zp1")
        a_wait(h, "zm0", table["A", "zm", h])
        a_sib(h, "zm0")

    def a_far(h):
        for k in (0, 1):
            a_wait(h, f"f{k}", table["A", "f", h] + k)
            a_sib(h, f"f{k}")

    def a_end(h):
        for i, kind in enumerate(a_kinds):
            arrived(fbuf.at[h, slab(a_slot(kind, 1 - co))], table["A", "sib", h] + i)

    def densify(first, last):
        @pl.loop(first, last)
        def _(c):
            pltpu.make_async_copy(tiles_ref.at[c], tbuf.at[c], tsem.at[c]).wait()
            for t in range(slots):
                rbuf[t] = tbuf[c, t].astype(F32) + rbuf[chain_ref[c, t]]
            for p in range(4 * NREP):
                r, k = p // 2, p % 2
                g, i = r // 2, r % 2
                row = ((g % 4 * 2 + g // 4) * 2 + i) * tile
                lane = pl.multiple_of(c * rows + k * tile, tile)
                adj[row:row + tile, pl.ds(lane, tile)] = rbuf[chain_ref[c, slots + p]].astype(BF16)

    def rows_of(x_):
        return pl.ds(pl.multiple_of(x_ * 2 * rows, 2 * rows), 2 * rows)

    def b_part(h, slot, x_):
        @pl.loop(0, 2)
        def _(i):
            where = pl.multiple_of(x_ * 2 * rows + i * rows, rows)
            pacc[slot, i] = jnp.dot(adj[pl.ds(where, rows), :], fbuf[h], preferred_element_type=F32)

    def b_first(h):
        b_part(h, 0, x2)
        bs2[h] = pacc[0].astype(BF16)
        send(bs2.at[h, 0], br2p.at[h], table["B", "2p", h], dev_xu)
        send(bs2.at[h, 1], br2m.at[h], table["B", "2m", h], dev_xd)

    def b_second(h):
        arrived(br2p.at[h], table["B", "2p", h])
        bsp[h, 0] = (pacc[1, 0] + br2p[h].astype(F32)).astype(BF16)
        bsp[h, 1] = pacc[1, 1].astype(BF16)
        send(bsp.at[h], brp.at[h], table["B", "p", h], dev_xu)
        arrived(br2m.at[h], table["B", "2m", h])
        bsm[h, 0] = pacc[2, 0].astype(BF16)
        bsm[h, 1] = (pacc[2, 1] + br2m[h].astype(F32)).astype(BF16)
        send(bsm.at[h], brm.at[h], table["B", "m", h], dev_xd)

    def b_third(h):
        arrived(brp.at[h], table["B", "p", h])
        arrived(brm.at[h], table["B", "m", h])
        other = 1 - yl
        bsy[h] = (pacc[3, other] + brp[h, other].astype(F32) + brm[h, other].astype(F32)).astype(BF16)
        send(bsy.at[h], bry.at[h], table["B", "y", h], dev_yl)
        pacc[3, yl] = pacc[3, yl] + brp[h, yl].astype(F32) + brm[h, yl].astype(F32)

    def b_fourth(h):
        arrived(bry.at[h], table["B", "y", h])
        agg[:, h * half:(h + 1) * half] = (pacc[3, yl] + bry[h].astype(F32)).astype(BF16)

    def d_slot(kind):
        x_, yl_ = {
            "own": (x, yl), "par": (x, 1 - yl), "xp0": (xd, 0), "xp1": (xd, 1),
            "xm0": (xu, 0), "xm1": (xu, 1), "f0": (x2, 0), "f1": (x2, 1),
        }[kind]
        return pl.ds(pl.multiple_of((x_ * 2 + yl_) * rows, rows), rows)

    def d_send(h, kind, number, dev, slot=None):
        block = gbuf.at[h, :, d_slot(kind)]
        send(block, block, number, dev, slot)

    def d_wait(h, kind, number):
        arrived(gbuf.at[h, :, d_slot(kind)], number)

    def d_own(h):
        d_send(h, "own", table["D", "y", h], dev_yl)
        d_send(h, "own", table["D", "xp", h], dev_xu, yl)
        d_send(h, "own", table["D", "xm", h], dev_xd, yl)

    def d_par(h):
        d_wait(h, "par", table["D", "y", h])
        d_send(h, "par", table["D", "xp", h], dev_xu, 1 - yl)
        d_send(h, "par", table["D", "xm", h], dev_xd, 1 - yl)

    def d_ring(h):
        d_wait(h, "xp0", table["D", "xp", h])
        d_send(h, "xp0", table["D", "f", h], dev_xu)
        d_wait(h, "xm1", table["D", "xm", h] + 1)
        d_send(h, "xm1", table["D", "f", h] + 1, dev_xd)
        d_wait(h, "xp1", table["D", "xp", h] + 1)
        d_wait(h, "xm0", table["D", "xm", h])

    def d_far(h):
        for k in (0, 1):
            d_wait(h, f"f{k}", table["D", "f", h] + k)

    zs = (z2, zu, zd, z)

    def e_part(h, kind):
        @pl.loop(0, 2)
        def _(i):
            there = did(zs[kind], i, 1 - co)
            here = did(zs[kind], i, co)
            ess[h, kind, i] = jnp.dot(
                gbuf[h], adj[:, slab(there)], preferred_element_type=F32).astype(BF16)
            eacc[kind, i] = jnp.dot(gbuf[h], adj[:, slab(here)], preferred_element_type=F32)

        for i in (0, 1):
            send(ess.at[h, kind, i], ers.at[h, kind, i], table["E", "sib", h] + kind * 2 + i, dev_sib)

    def e_joined(h, kind, i):
        arrived(ers.at[h, kind, i], table["E", "sib", h] + kind * 2 + i)
        return eacc[kind, i] + ers[h, kind, i].astype(F32)

    def e_first(h):
        es2[h, 0] = e_joined(h, 0, 0).astype(BF16)
        send(es2.at[h, 0], er2p.at[h], table["E", "2p", h], dev_zu)
        es2[h, 1] = e_joined(h, 0, 1).astype(BF16)
        send(es2.at[h, 1], er2m.at[h], table["E", "2m", h], dev_zd)

    def e_second(h):
        esp[h, 1] = e_joined(h, 1, 1).astype(BF16)
        send(esp.at[h, 1], erp.at[h, 1], table["E", "p", h] + 1, dev_zu)
        esm[h, 0] = e_joined(h, 2, 0).astype(BF16)
        send(esm.at[h, 0], erm.at[h, 0], table["E", "m", h], dev_zd)
        value = e_joined(h, 1, 0)
        arrived(er2p.at[h], table["E", "2p", h])
        esp[h, 0] = (value + er2p[h].astype(F32)).astype(BF16)
        send(esp.at[h, 0], erp.at[h, 0], table["E", "p", h], dev_zu)
        value = e_joined(h, 2, 1)
        arrived(er2m.at[h], table["E", "2m", h])
        esm[h, 1] = (value + er2m[h].astype(F32)).astype(BF16)
        send(esm.at[h, 1], erm.at[h, 1], table["E", "m", h] + 1, dev_zd)

    def e_third(h):
        for i in (0, 1):
            eacc[3, i] = e_joined(h, 3, i)
        for i in (0, 1):
            arrived(erp.at[h, i], table["E", "p", h] + i)
            arrived(erm.at[h, i], table["E", "m", h] + i)
        other = 1 - yh
        esy[h] = (eacc[3, other] + erp[h, other].astype(F32) + erm[h, other].astype(F32)).astype(BF16)
        send(esy.at[h], ery.at[h], table["E", "y", h], dev_yp)
        eacc[3, yh] = eacc[3, yh] + erp[h, yh].astype(F32) + erm[h, yh].astype(F32)

    def e_fourth(h):
        arrived(ery.at[h], table["E", "y", h])
        total = eacc[3, yh] + ery[h].astype(F32)
        fgrad_ref[:, h * half:(h + 1) * half] = total.T.astype(BF16)

    wc, wz, wy = width // 2, width // 8, width // 32
    wl = width // 4

    def at(i, n):
        return pl.ds(pl.multiple_of(i * n, n), n)

    def w_core():
        send(wpart.at[at(1 - co, wc)], wrc, table["W", "rc"], dev_sib)

    def w_z():
        arrived(wrc, table["W", "rc"])
        wpart[at(co, wc)] = wpart[at(co, wc)] + wrc[...]
        wzb[...] = wpart[at(co, wc)].astype(BF16)
        for k in (1, 2, 3):
            send(wzb.at[at(turn(z, k), wz)], wrz.at[k - 1], table["W", "rz"] + k - 1, zpeers[k - 1])

    def w_y():
        w2[...] = wpart[pl.ds(pl.multiple_of(co * wc + z * wz, wz), wz)]
        for k in range(3):
            arrived(wrz.at[k], table["W", "rz"] + k)
            w2[...] += wrz[k].astype(F32)
        for k in (1, 2, 3):
            send(w2.at[at(turn(y, k), wy)], wry.at[k - 1], table["W", "ry"] + k - 1, ypeers[k - 1])

    def w_x():
        total = w2[at(y, wy)]
        for k in range(3):
            arrived(wry.at[k], table["W", "ry"] + k)
            total = total + wry[k]
        w3[...] = total
        for k in (1, 2, 3):
            send(w3.at[:, at(turn(x, k), wl)], wrx.at[k - 1], table["W", "rx"] + k - 1, xpeers[k - 1])

    first_z = pl.ds(pl.multiple_of(co * wc + z * wz, wz), wz)

    def row_at(y_):
        return pl.ds(pl.multiple_of(co * wc + z * wz + y_ * wy, wy), wy)

    def w_gx():
        total = w3[:, at(x, wl)]
        for k in range(3):
            arrived(wrx.at[k], table["W", "rx"] + k)
            total = total + wrx[k]
        wfull[row_at(y), at(x, wl)] = total.astype(BF16)
        block = wfull.at[row_at(y), at(x, wl)]
        for k in range(3):
            send(block, block, table["W", "gx"] + k, xpeers[k])

    def w_gy():
        for k in (1, 2, 3):
            arrived(wfull.at[row_at(y), at(turn(x, 4 - k), wl)], table["W", "gx"] + k - 1)
        block = wfull.at[row_at(y)]
        for k in range(3):
            send(block, block, table["W", "gy"] + k, ypeers[k])

    def w_gz():
        for k in (1, 2, 3):
            arrived(wfull.at[row_at(turn(y, 4 - k))], table["W", "gy"] + k - 1)
        block = wfull.at[first_z]
        for k in range(3):
            send(block, block, table["W", "gz"] + k, zpeers[k])

    def w_gc():
        for k in (1, 2, 3):
            where = pl.multiple_of(co * wc + turn(z, 4 - k) * wz, wz)
            arrived(wfull.at[pl.ds(where, wz)], table["W", "gz"] + k - 1)
        block = wfull.at[at(co, wc)]
        send(block, block, table["W", "gc"], dev_sib)

    def w_end():
        arrived(wfull.at[at(1 - co, wc)], table["W", "gc"])
        wgrad_ref[...] = wfull[...].astype(F32) * scale

    a_own(0)
    a_own(1)
    densify(0, 6)
    a_par(0)
    densify(6, 10)
    a_par(1)
    a_ring(0)
    densify(10, NDOM)
    a_ring(1)
    a_far(0)
    a_end(0)
    b_first(0)
    b_part(0, 1, xu)
    b_part(0, 2, xd)
    a_far(1)
    b_part(0, 3, x)
    b_second(0)
    a_end(1)
    b_third(0)
    b_first_1 = lambda: b_first(1)
    b_fourth(0)
    b_first_1()
    b_part(1, 1, xu)
    b_part(1, 2, xd)
    b_second(1)
    b_part(1, 3, x)
    b_third(1)
    b_fourth(1)

    preact[...] = jnp.dot(agg[...], w_ref[...], preferred_element_type=F32)
    pre = preact[...]
    sig = 1.0 / (1.0 + jnp.exp(-pre))
    act_ref[...] = (pre * sig).astype(BF16)
    grad = (cot_ref[...].astype(F32) * (sig * (1.0 + pre * (1.0 - sig)))).astype(BF16)
    for h in (0, 1):
        gbuf[h, :, d_slot("own")] = lax.dot_general(
            w_ref[h * half:(h + 1) * half, :], grad, (((1,), (1,)), ((), ())),
            preferred_element_type=F32).astype(BF16)
        d_own(h)
    wpart[...] = lax.dot_general(
        agg[...], grad, (((0,), (0,)), ((), ())), preferred_element_type=F32)
    w_core()

    d_par(0)
    d_par(1)
    w_z()
    d_ring(0)
    d_ring(1)
    d_far(0)
    e_part(0, 0)
    w_y()
    e_part(0, 1)
    e_first(0)
    d_far(1)
    e_part(0, 2)
    w_x()
    e_part(0, 3)
    e_second(0)
    e_part_1 = lambda kind: e_part(1, kind)
    w_gx()
    e_third(0)
    w_gy()
    e_fourth(0)
    e_part_1(0)
    e_part_1(1)
    e_first(1)
    w_gz()
    e_part_1(2)
    e_part_1(3)
    e_second(1)
    w_gc()
    e_third(1)
    w_end()
    e_fourth(1)
    for copy in pending:
        copy.wait_send()


def local(features, cotangent, weight, tiles, tile_rows, tile_cols, tile_counts):
    rows, width = features.shape
    slots, tile = tiles.shape[3], tiles.shape[-1]
    half = width // 2
    place = tile_rows[0, 0] * 2 + tile_cols[0, 0]
    order = jnp.arange(slots, dtype=jnp.int32)
    target = jnp.concatenate(
        [place, jnp.broadcast_to(jnp.arange(4 * NREP, dtype=jnp.int32), (NDOM, 4 * NREP))], axis=1)
    limit = jnp.concatenate([order, jnp.full((4 * NREP,), slots, jnp.int32)])
    limit = jnp.minimum(limit[None, :], tile_counts[0, 0][:, None])
    match = (place[:, None, :] == target[:, :, None]) & (order[None, None, :] < limit[:, :, None])
    chain = jnp.max(jnp.where(match, order[None, None, :], -1), axis=2)
    chain = jnp.where(chain < 0, slots, chain)

    table, count = message_table()
    dims = (rows, width, tile, slots)
    vmem = pltpu.VMEM
    scratch = [
        vmem((NDOM, slots, tile, tile), BF16),
        vmem((slots + 1, tile, tile), F32),
        vmem((NREP * rows, NDOM * rows), BF16),
        vmem((2, NDOM * rows, half), BF16),
        vmem((2, half, NREP * rows), BF16),
        vmem((4, 2, rows, half), F32),
        vmem((4, 2, half, rows), F32),
        vmem((rows, width), BF16),
        vmem((rows, width), F32),
        vmem((2, 2, rows, half), BF16),
        vmem((2, 2, rows, half), BF16),
        vmem((2, 2, rows, half), BF16),
        vmem((2, rows, half), BF16),
        vmem((2, rows, half), BF16),
        vmem((2, rows, half), BF16),
        vmem((2, 2, rows, half), BF16),
        vmem((2, 2, rows, half), BF16),
        vmem((2, rows, half), BF16),
        vmem((2, 4, 2, half, rows), BF16),
        vmem((2, 2, half, rows), BF16),
        vmem((2, 2, half, rows), BF16),
        vmem((2, 2, half, rows), BF16),
        vmem((2, half, rows), BF16),
        vmem((2, 4, 2, half, rows), BF16),
        vmem((2, half, rows), BF16),
        vmem((2, half, rows), BF16),
        vmem((2, 2, half, rows), BF16),
        vmem((2, 2, half, rows), BF16),
        vmem((2, half, rows), BF16),
        vmem((width, width), F32),
        vmem((width // 2, width), F32),
        vmem((width // 2, width), BF16),
        vmem((3, width // 8, width), BF16),
        vmem((width // 8, width), F32),
        vmem((3, width // 32, width), F32),
        vmem((width // 32, width), F32),
        vmem((3, width // 32, width // 4), F32),
        vmem((width, width), BF16),
        pltpu.SemaphoreType.DMA((NDOM,)),
        pltpu.SemaphoreType.DMA((2,)),
        pltpu.SemaphoreType.DMA((count,)),
        pltpu.SemaphoreType.DMA((count,)),
    ]
    whole = pl.BlockSpec(memory_space=pltpu.VMEM)
    anywhere = pl.BlockSpec(memory_space=pl.ANY)
    return pl.pallas_call(
        functools.partial(kernel, dims, table),
        out_shape=(
            jax.ShapeDtypeStruct((rows, width), BF16),
            jax.ShapeDtypeStruct((rows, width), BF16),
            jax.ShapeDtypeStruct((width, width), F32),
        ),
        in_specs=[pl.BlockSpec(memory_space=pltpu.SMEM), anywhere, whole, whole, anywhere],
        out_specs=(whole, whole, whole),
        scratch_shapes=scratch,
        compiler_params=pltpu.CompilerParams(
            collective_id=0, has_side_effects=True, vmem_limit_bytes=67043328),
    )(chain, features, cotangent, weight, tiles[0, 0])


def solution(mesh):
    in_specs = (
        P(("dom", "repl"), None),
        P(("dom", "repl"), None),
        P(),
        P("dom", "repl", None, None, None, None),
        P("dom", "repl", None, None),
        P("dom", "repl", None, None),
        P("dom", "repl", None),
    )
    out_specs = (P(("dom", "repl"), None), P(("dom", "repl"), None), P())
    return jax.shard_map(local, mesh=mesh, in_specs=in_specs, out_specs=out_specs, check_vma=False)
```

```python
import functools

import jax
import jax.numpy as jnp
from jax import lax
from jax.experimental import pallas as pl
from jax.experimental.pallas import tpu as pltpu
from jax.sharding import PartitionSpec as P

F32 = jnp.float32
BF16 = jnp.bfloat16
MESH = pl.DeviceIdType.MESH
Z, YH, CO, YL, X = 4, 2, 2, 2, 4
NDOM, NREP = Z * YH * CO, YL * X
VMEM_LIMIT = 60 << 20


class Names:
    def __init__(self):
        self.count = 0

    def take(self, n=1):
        base = self.count
        self.count += n
        return base


def message_table():
    names = Names()
    table = {}
    gather = ("y0", "y1", "nu0", "nu1", "nd0", "nd1", "fu", "fd", "hd", "hu", "pu", "pd", "qu", "qd")
    reduce = ("f0u", "f0d", "f1u", "f1d", "yu", "yd", "tu", "td", "ou0", "ou1", "od0", "od1", "y0", "y1")
    for h in (0, 1):
        for phase, kinds, siblings in (("A", gather, 8), ("B", reduce, 0), ("D", gather, 0), ("E", reduce, 8)):
            for kind in kinds:
                table[phase, kind, h] = names.take()
            if siblings:
                table[phase, "sib", h] = names.take(siblings)
    for kind in ("rc", "gc"):
        table["W", kind] = names.take(1)
    for kind in ("rz", "ry", "rx", "gx", "gy", "gz"):
        table["W", kind] = names.take(3)
    return table, names.count


def kernel(dims, table, trow_ref, tcol_ref, count_ref, feat_ref, cot_ref, w_ref, tiles_ref,
           act_ref, grad_ref, wgrad_ref, *scratch):
    rows, width, tile, slots = dims
    half = width // 2
    (tbuf, rbuf, adj, fbuf, gbuf, pacc, eacc, agg, preact,
     bs_far, bs_y0, bs_t, bs_o, bs_y, br_far, br_y0, br_t, br_o, br_y,
     es_far, es_y0, es_t, es_o, es_y, er_far, er_y0, er_t, er_o, er_y, ess, ers,
     wpart, wrc, wzb, wrz, w2, wry, w3, wrx, wfull,
     wanted, links, chain_ref,
     tsem, fsem, csem, ssem, rsem) = scratch

    dom = lax.axis_index("dom")
    rep = lax.axis_index("repl")
    co = lax.rem(dom, 2)
    yh = lax.rem(lax.div(dom, 2), 2)
    z = lax.div(dom, 4)
    x = lax.rem(rep, 4)
    yl = lax.div(rep, 4)
    y = yh * 2 + yl

    def turn(v, by):
        return lax.rem(v + by, 4)

    zu, zd, z2 = turn(z, 1), turn(z, 3), turn(z, 2)
    xu, xd, x2 = turn(x, 1), turn(x, 3), turn(x, 2)

    def did(z_, yh_, co_):
        return z_ * 4 + yh_ * 2 + co_

    def at_y(y_):
        return (did(z, lax.div(y_, 2), co), lax.rem(y_, 2) * 4 + x)

    dev_sib = (did(z, yh, 1 - co), rep)
    dev_zu, dev_zd = (did(zu, yh, co), rep), (did(zd, yh, co), rep)
    dev_yp = (did(z, 1 - yh, co), rep)
    dev_xu, dev_xd = (dom, yl * 4 + xu), (dom, yl * 4 + xd)
    dev_yl = (dom, (1 - yl) * 4 + x)
    zpeers = [(did(turn(z, k), yh, co), rep) for k in (1, 2, 3)]
    ypeers = [at_y(turn(y, k)) for k in (1, 2, 3)]
    xpeers = [(dom, yl * 4 + turn(x, k)) for k in (1, 2, 3)]

    pending = []

    def send(src, dst, number, dev, slot=None):
        arrival = number if slot is None else number + slot
        copy = pltpu.make_async_remote_copy(
            src_ref=src, dst_ref=dst, send_sem=ssem.at[len(pending)], recv_sem=rsem.at[arrival],
            device_id=dev, device_id_type=MESH)
        copy.start()
        pending.append(copy)

    def arrived(dst, number, slot=None):
        number = number if slot is None else number + slot
        pltpu.make_async_remote_copy(
            src_ref=dst, dst_ref=dst, send_sem=ssem.at[0], recv_sem=rsem.at[number],
            device_id=dev_sib, device_id_type=MESH).wait_recv()

    def slab(c):
        return pl.ds(pl.multiple_of(c * rows, rows), rows)

    for h in (0, 1):
        pltpu.make_async_copy(
            feat_ref.at[:, h * half:(h + 1) * half], fbuf.at[h, slab(dom)], fsem.at[h]).start()
    for c in range(NDOM):
        pltpu.make_async_copy(tiles_ref.at[c], tbuf.at[c], tsem.at[c]).start()
    barrier = pltpu.get_barrier_semaphore()
    partners = [dev_sib] + zpeers + ypeers + xpeers
    for dev in partners:
        pl.semaphore_signal(barrier, inc=1, device_id=dev, device_id_type=MESH)
    rbuf[slots] = jnp.zeros((tile, tile), F32)

    place = trow_ref[...] * 2 + tcol_ref[...]
    lane = lax.broadcasted_iota(jnp.int32, (NDOM, 128), 1)
    wanted[...] = lane - slots
    wanted[:, :slots] = place
    target = wanted[...]
    square = (NDOM, NDOM)
    diagonal = lax.broadcasted_iota(jnp.int32, square, 0) == lax.broadcasted_iota(jnp.int32, square, 1)
    live = jnp.sum(jnp.where(diagonal, count_ref[...], 0), axis=1, keepdims=True)
    limit = jnp.minimum(jnp.where(lane < slots, lane, slots), live)
    chain = jnp.full((NDOM, 128), slots, jnp.int32)
    for t in range(slots):
        chain = jnp.where((target == place[:, t:t + 1]) & (t < limit), t, chain)
    links[...] = chain
    pl.semaphore_wait(barrier, len(partners))
    load = pltpu.make_async_copy(links, chain_ref, csem)
    load.start()

    def part_of(n, part):
        return pl.ds(0, n) if part is None else pl.ds(part * (n // 2), n // 2)

    def gather(phase, view, dev_u, dev_d, dev_y, after):
        def push(h, kind, dev, *where):
            block = view(h, *where)
            send(block, block, table[phase, kind, h], dev)

        def wait(h, kind, *where):
            arrived(view(h, *where), table[phase, kind, h])

        def pair(h):
            for part in (0, 1):
                push(h, f"y{part}", dev_y, "me", 1, part)
            after(h, "me", 1)

        def near(h, turn_):
            push(h, f"nu{turn_}", dev_u, "me", 1, turn_)
            push(h, f"nd{1 - turn_}", dev_d, "me", 1, 1 - turn_)

        def far(h):
            wait(h, "nu0", "d", 1, 0)
            push(h, "fu", dev_u, "d", 1, 0)
            wait(h, "nd1", "u", 1, 1)
            push(h, "fd", dev_d, "u", 1, 1)

        def side(h):
            wait(h, "nu1", "d", 1, 1)
            push(h, "hd", dev_y, "d", 1, 1)
            wait(h, "nd0", "u", 1, 0)
            push(h, "hu", dev_y, "u", 1, 0)
            after(h, "d", 1)
            after(h, "u", 1)

        def other(h):
            wait(h, "y0", "me", 0, 0)
            push(h, "pu", dev_u, "me", 0, 0)
            wait(h, "y1", "me", 0, 1)
            push(h, "pd", dev_d, "me", 0, 1)
            after(h, "me", 0)

        def far_other(h):
            wait(h, "pu", "d", 0, 0)
            push(h, "qu", dev_u, "d", 0, 0)
            wait(h, "pd", "u", 0, 1)
            push(h, "qd", dev_d, "u", 0, 1)

        def rest(h):
            wait(h, "hd", "d", 0, 1)
            wait(h, "hu", "u", 0, 0)
            after(h, "d", 0)
            after(h, "u", 0)
            wait(h, "fu", "2", 1, 0)
            wait(h, "fd", "2", 1, 1)
            after(h, "2", 1)
            wait(h, "qu", "2", 0, 0)
            wait(h, "qd", "2", 0, 1)
            after(h, "2", 0)

        return pair, near, far, side, other, far_other, rest

    FAR, UP, DOWN, HERE = 0, 1, 2, 3

    def reduce(phase, n, value, acc, buffers, dev_u, dev_d, dev_y):
        s_far, s_y0, s_t, s_o, s_y, r_far, r_y0, r_t, r_o, r_y = buffers
        a, b = part_of(n, 0), part_of(n, 1)

        def push(src, dst, h, kind, dev):
            send(src, dst, table[phase, kind, h], dev)

        def far(h):
            for q in (0, 1):
                s_far[h, q] = value(h, FAR, q, part_of(n, None)).astype(BF16)
                push(s_far.at[h, q, a], r_far.at[h, q, 0], h, f"f{q}u", dev_u)
                push(s_far.at[h, q, b], r_far.at[h, q, 1], h, f"f{q}d", dev_d)

        def pair_up(h):
            s_y0[h, 0] = value(h, UP, 0, b).astype(BF16)
            push(s_y0.at[h, 0], r_y0.at[h, 0], h, "yu", dev_y)

        def pair_down(h):
            s_y0[h, 1] = value(h, DOWN, 0, a).astype(BF16)
            push(s_y0.at[h, 1], r_y0.at[h, 1], h, "yd", dev_y)

        def other(h):
            above, below = value(h, UP, 0, a), value(h, DOWN, 0, b)
            arrived(r_far.at[h, 0, 0], table[phase, "f0u", h])
            s_t[h, 0] = (above + r_far[h, 0, 0].astype(F32)).astype(BF16)
            push(s_t.at[h, 0], r_t.at[h, 0], h, "tu", dev_u)
            arrived(r_far.at[h, 0, 1], table[phase, "f0d", h])
            s_t[h, 1] = (below + r_far[h, 0, 1].astype(F32)).astype(BF16)
            push(s_t.at[h, 1], r_t.at[h, 1], h, "td", dev_d)

        def own(h):
            for i, (kind, dev, name, one, two) in enumerate(((UP, dev_u, "u", a, b), (DOWN, dev_d, "d", b, a))):
                value_one, value_two = value(h, kind, 1, one), value(h, kind, 1, two)
                arrived(r_far.at[h, 1, i], table[phase, f"f1{name}", h])
                s_o[h, i, one] = (value_one + r_far[h, 1, i].astype(F32)).astype(BF16)
                push(s_o.at[h, i, one], r_o.at[h, i, one], h, f"o{name}0", dev)
                arrived(r_y0.at[h, i], table[phase, f"y{name}", h])
                s_o[h, i, two] = (value_two + r_y0[h, i].astype(F32)).astype(BF16)
                push(s_o.at[h, i, two], r_o.at[h, i, two], h, f"o{name}1", dev)

        def pair(h):
            for i, (name, rows_) in enumerate((("u", a), ("d", b))):
                arrived(r_t.at[h, i], table[phase, f"t{name}", h])
                s_y[h, rows_] = (value(h, HERE, 0, rows_) + r_t[h, i].astype(F32)).astype(BF16)
                push(s_y.at[h, rows_], r_y.at[h, rows_], h, f"y{i}", dev_y)

        def collect(h):
            total = value(h, HERE, 1, part_of(n, None))
            for i, (name, one, two) in enumerate((("u", a, b), ("d", b, a))):
                arrived(r_o.at[h, i, one], table[phase, f"o{name}0", h])
                arrived(r_o.at[h, i, two], table[phase, f"o{name}1", h])
            acc[h, HERE, 1] = total + r_o[h, 0].astype(F32) + r_o[h, 1].astype(F32)

        def end(h):
            arrived(r_y.at[h, a], table[phase, "y0", h])
            arrived(r_y.at[h, b], table[phase, "y1", h])
            return acc[h, HERE, 1] + r_y[h].astype(F32)

        return far, pair_up, pair_down, other, own, pair, collect, end

    a_places = [("me", 1), ("me", 0), ("d", 1), ("u", 1), ("d", 0), ("u", 0), ("2", 1), ("2", 0)]

    def a_slot(place, column, core):
        return did({"me": z, "u": zu, "d": zd, "2": z2}[place], yh if column else 1 - yh, core)

    def a_view(h, place, column, part):
        start = a_slot(place, column, co) * rows + (0 if part is None else part * (rows // 2))
        size = rows if part is None else rows // 2
        return fbuf.at[h, pl.ds(pl.multiple_of(start, size), size)]

    def a_after(h, place, column):
        block = a_view(h, place, column, None)
        send(block, block, table["A", "sib", h] + a_places.index((place, column)), dev_sib)

    a_pair, a_near, a_far, a_side, a_other, a_far_other, a_rest = gather("A", a_view, dev_zu, dev_zd, dev_yp, a_after)

    def a_open(h):
        pltpu.make_async_copy(
            feat_ref.at[:, h * half:(h + 1) * half], fbuf.at[h, slab(dom)], fsem.at[h]).wait()
        a_pair(h)

    def a_end(h):
        for i, (place, column) in enumerate(a_places):
            arrived(fbuf.at[h, slab(a_slot(place, column, 1 - co))], table["A", "sib", h] + i)

    def densify(first, last):
        @pl.loop(first, last)
        def _(c):
            pltpu.make_async_copy(tiles_ref.at[c], tbuf.at[c], tsem.at[c]).wait()
            for t in range(slots):
                rbuf[t] = tbuf[c, t].astype(F32) + rbuf[chain_ref[c, t]]
            for p in range(4 * NREP):
                r, k = p // 2, p % 2
                g, i = r // 2, r % 2
                row = ((g % 4 * 2 + g // 4) * 2 + i) * tile
                lane = pl.multiple_of(c * rows + k * tile, tile)
                adj[row:row + tile, pl.ds(lane, tile)] = rbuf[chain_ref[c, slots + p]].astype(BF16)

    def b_part(h, kind):
        x_ = (x2, xu, xd, x)[kind]

        @pl.loop(0, 2)
        def _(i):
            parity = i * yl + (1 - i) * (1 - yl)
            where = pl.multiple_of((x_ * 2 + parity) * rows, rows)
            pacc[h, kind, i] = jnp.dot(adj[pl.ds(where, rows), :], fbuf[h], preferred_element_type=F32)

    def b_value(h, kind, q, part):
        return pacc[h, kind, q, part]

    b_far, b_pair_up, b_pair_down, b_other, b_own, b_pair, b_collect, b_end = reduce(
        "B", rows, b_value, pacc, (bs_far, bs_y0, bs_t, bs_o, bs_y, br_far, br_y0, br_t, br_o, br_y),
        dev_xu, dev_xd, dev_yl)

    def b_close(h):
        agg[:, h * half:(h + 1) * half] = b_end(h).astype(BF16)

    def d_view(h, place, column, part):
        slot = {"me": x, "u": xu, "d": xd, "2": x2}[place] * 2 + (yl if column else 1 - yl)
        return gbuf.at[h, part_of(half, part), pl.ds(pl.multiple_of(slot * rows, rows), rows)]

    d_pair, d_near, d_far, d_side, d_other, d_far_other, d_rest = gather(
        "D", d_view, dev_xu, dev_xd, dev_yl, lambda h, place, column: None)

    def e_part(h, kind):
        z_ = (z2, zu, zd, z)[kind]

        @pl.loop(0, 2)
        def _(i):
            parity = i * yh + (1 - i) * (1 - yh)
            ess[h, kind, i] = jnp.dot(
                gbuf[h], adj[:, slab(did(z_, parity, 1 - co))], preferred_element_type=F32).astype(BF16)
            eacc[h, kind, i] = jnp.dot(
                gbuf[h], adj[:, slab(did(z_, parity, co))], preferred_element_type=F32)

        for i in (0, 1):
            send(ess.at[h, kind, i], ers.at[h, kind, i], table["E", "sib", h] + kind * 2 + i, dev_sib)

    def e_join(h, kind):
        for i in (0, 1):
            arrived(ers.at[h, kind, i], table["E", "sib", h] + kind * 2 + i)

    def e_value(h, kind, q, part):
        return eacc[h, kind, q, part] + ers[h, kind, q, part].astype(F32)

    e_far, e_pair_up, e_pair_down, e_other, e_own, e_pair, e_collect, e_end = reduce(
        "E", half, e_value, eacc, (es_far, es_y0, es_t, es_o, es_y, er_far, er_y0, er_t, er_o, er_y),
        dev_zu, dev_zd, dev_yp)

    def e_close(h):
        grad_ref[h * half:(h + 1) * half, :] = e_end(h).astype(BF16)

    wc, wz, wy = width // 2, width // 8, width // 32
    wl = width // 4

    def at(i, n):
        return pl.ds(pl.multiple_of(i * n, n), n)

    def w_core():
        send(wpart.at[at(1 - co, wc)], wrc, table["W", "rc"], dev_sib)

    def first_at(y_):
        return pl.ds(pl.multiple_of(co * wc + y_ * wz, wz), wz)

    def row_at(z_):
        return pl.ds(pl.multiple_of(co * wc + y * wz + z_ * wy, wy), wy)

    def w_y():
        arrived(wrc, table["W", "rc"])
        wpart[at(co, wc)] = wpart[at(co, wc)] + wrc[...]
        wzb[...] = wpart[at(co, wc)].astype(BF16)
        for k in (1, 2, 3):
            send(wzb.at[at(turn(y, k), wz)], wrz.at[k - 1], table["W", "ry"] + k - 1, ypeers[k - 1])

    def w_z():
        w2[...] = wpart[first_at(y)]
        for k in range(3):
            arrived(wrz.at[k], table["W", "ry"] + k)
            w2[...] += wrz[k].astype(F32)
        for k in (1, 2, 3):
            send(w2.at[at(turn(z, k), wy)], wry.at[k - 1], table["W", "rz"] + k - 1, zpeers[k - 1])

    def w_x():
        total = w2[at(z, wy)]
        for k in range(3):
            arrived(wry.at[k], table["W", "rz"] + k)
            total = total + wry[k]
        w3[...] = total
        for k in (1, 2, 3):
            send(w3.at[:, at(turn(x, k), wl)], wrx.at[k - 1], table["W", "rx"] + k - 1, xpeers[k - 1])

    def w_gx():
        total = w3[:, at(x, wl)]
        for k in range(3):
            arrived(wrx.at[k], table["W", "rx"] + k)
            total = total + wrx[k]
        wfull[row_at(z), at(x, wl)] = total.astype(BF16)
        block = wfull.at[row_at(z), at(x, wl)]
        for k in range(3):
            send(block, block, table["W", "gx"] + k, xpeers[k])

    def w_gz():
        for k in (1, 2, 3):
            arrived(wfull.at[row_at(z), at(turn(x, 4 - k), wl)], table["W", "gx"] + k - 1)
        block = wfull.at[row_at(z)]
        for k in range(3):
            send(block, block, table["W", "gz"] + k, zpeers[k])

    def w_gy():
        for k in (1, 2, 3):
            arrived(wfull.at[row_at(turn(z, 4 - k))], table["W", "gz"] + k - 1)
        block = wfull.at[first_at(y)]
        for k in range(3):
            send(block, block, table["W", "gy"] + k, ypeers[k])

    def w_gc():
        for k in (1, 2, 3):
            arrived(wfull.at[first_at(turn(y, 4 - k))], table["W", "gy"] + k - 1)
        block = wfull.at[at(co, wc)]
        send(block, block, table["W", "gc"], dev_sib)

    def w_end():
        arrived(wfull.at[at(1 - co, wc)], table["W", "gc"])
        wgrad_ref[...] = wfull[...]

    a_open(0)
    a_near(0, 0)
    a_near(0, 1)
    a_open(1)
    a_near(1, 0)
    load.wait()
    densify(0, 6)
    a_far(0)
    a_other(0)
    a_near(1, 1)
    a_side(0)
    densify(6, 10)
    a_other(1)
    a_far_other(0)
    a_far(1)
    a_side(1)
    densify(10, NDOM)
    a_far_other(1)
    a_rest(0)
    a_end(0)
    b_part(0, FAR)
    b_far(0)
    b_part(0, UP)
    b_pair_up(0)
    a_rest(1)
    b_part(0, DOWN)
    b_pair_down(0)
    a_end(1)
    b_other(0)
    b_part(1, FAR)
    b_far(1)
    b_own(0)
    b_part(1, UP)
    b_pair_up(1)
    b_part(1, DOWN)
    b_pair_down(1)
    b_part(0, HERE)
    b_pair(0)
    b_other(1)
    b_part(1, HERE)
    b_own(1)
    b_collect(0)
    b_pair(1)
    b_close(0)
    preact[...] = jnp.dot(agg[:, :half], w_ref[:half, :], preferred_element_type=F32)
    b_collect(1)
    b_close(1)

    pre = preact[...] + jnp.dot(agg[:, half:], w_ref[half:, :], preferred_element_type=F32)
    sig = 1.0 / (1.0 + jnp.exp(-pre))
    act_ref[...] = (pre * sig).astype(BF16)
    grad = (cot_ref[...].astype(F32) * (sig * (1.0 + pre * (1.0 - sig)))).astype(BF16)
    for h in (0, 1):
        gbuf[h, :, pl.ds(pl.multiple_of((x * 2 + yl) * rows, rows), rows)] = lax.dot_general(
            w_ref[h * half:(h + 1) * half, :], grad, (((1,), (1,)), ((), ())),
            preferred_element_type=F32).astype(BF16)
        d_pair(h)
        d_near(h, 0)
        if h == 0:
            d_near(h, 1)
    wpart[...] = lax.dot_general(
        agg[...], grad, (((0,), (0,)), ((), ())), preferred_element_type=F32)
    w_core()

    d_far(0)
    d_other(0)
    d_near(1, 1)
    d_side(0)
    w_y()
    d_other(1)
    d_far_other(0)
    d_far(1)
    d_side(1)
    w_z()
    d_far_other(1)
    d_rest(0)
    e_part(0, FAR)
    e_part(0, UP)
    e_join(0, FAR)
    e_far(0)
    w_x()
    e_part(0, DOWN)
    e_join(0, UP)
    e_pair_up(0)
    d_rest(1)
    e_part(1, FAR)
    e_join(0, DOWN)
    e_pair_down(0)
    e_other(0)
    e_part(1, UP)
    e_join(1, FAR)
    e_far(1)
    w_gx()
    e_own(0)
    e_part(1, DOWN)
    e_join(1, UP)
    e_pair_up(1)
    w_gz()
    e_part(0, HERE)
    e_join(1, DOWN)
    e_pair_down(1)
    e_other(1)
    e_join(0, HERE)
    e_pair(0)
    e_part(1, HERE)
    w_gy()
    e_own(1)
    e_join(1, HERE)
    e_pair(1)
    e_collect(0)
    w_gc()
    e_close(0)
    e_collect(1)
    w_end()
    e_close(1)
    for copy in pending:
        copy.wait_send()


def reduce_scratch(n, m):
    shapes = [
        [(2, 2, n, m), (2, 2, n // 2, m), (2, 2, n // 2, m), (2, 2, n, m), (2, n, m)],
        [(2, 2, 2, n // 2, m), (2, 2, n // 2, m), (2, 2, n // 2, m), (2, 2, n, m), (2, n, m)],
    ]
    return [pltpu.VMEM(shape, BF16) for side in shapes for shape in side]


def finish(scale, act_ref, grad_t_ref, weight_ref, act_out, fgrad_out, wgrad_out):
    act_out[...] = act_ref[...]
    fgrad_out[...] = grad_t_ref[...].T
    wgrad_out[...] = weight_ref[...].astype(F32) * scale


def local(features, cotangent, weight, tiles, tile_rows, tile_cols, tile_counts):
    rows, width = features.shape
    slots, tile = tiles.shape[3], tiles.shape[-1]
    half = width // 2
    table, count = message_table()
    dims = (rows, width, tile, slots)
    vmem = pltpu.VMEM
    scratch = [
        vmem((NDOM, slots, tile, tile), BF16),
        vmem((slots + 1, tile, tile), F32),
        vmem((NREP * rows, NDOM * rows), BF16),
        vmem((2, NDOM * rows, half), BF16),
        vmem((2, half, NREP * rows), BF16),
        vmem((2, 4, 2, rows, half), F32),
        vmem((2, 4, 2, half, rows), F32),
        vmem((rows, width), BF16),
        vmem((rows, width), F32),
        *reduce_scratch(rows, half),
        *reduce_scratch(half, rows),
        vmem((2, 4, 2, half, rows), BF16),
        vmem((2, 4, 2, half, rows), BF16),
        vmem((width, width), F32),
        vmem((width // 2, width), F32),
        vmem((width // 2, width), BF16),
        vmem((3, width // 8, width), BF16),
        vmem((width // 8, width), F32),
        vmem((3, width // 32, width), F32),
        vmem((width // 32, width), F32),
        vmem((3, width // 32, width // 4), F32),
        vmem((width, width), BF16),
        vmem((NDOM, 128), jnp.int32),
        vmem((NDOM, 128), jnp.int32),
        pltpu.SMEM((NDOM, 128), jnp.int32),
        pltpu.SemaphoreType.DMA((NDOM,)),
        pltpu.SemaphoreType.DMA((2,)),
        pltpu.SemaphoreType.DMA,
        pltpu.SemaphoreType.DMA((count,)),
        pltpu.SemaphoreType.DMA((count,)),
    ]
    whole = pl.BlockSpec(memory_space=pltpu.VMEM)
    anywhere = pl.BlockSpec(memory_space=pl.ANY)
    act, grad_t, weight_sum = pl.pallas_call(
        functools.partial(kernel, dims, table),
        out_shape=(
            jax.ShapeDtypeStruct((rows, width), BF16),
            jax.ShapeDtypeStruct((width, rows), BF16),
            jax.ShapeDtypeStruct((width, width), BF16),
        ),
        in_specs=[whole, whole, whole, anywhere, whole, whole, anywhere],
        out_specs=(whole, whole, whole),
        scratch_shapes=scratch,
        compiler_params=pltpu.CompilerParams(
            collective_id=0, has_side_effects=True, vmem_limit_bytes=VMEM_LIMIT),
    )(tile_rows[0, 0], tile_cols[0, 0], tile_counts[0], features, cotangent, weight, tiles[0, 0])
    return pl.pallas_call(
        functools.partial(finish, float(rows * NDOM * NREP) ** (-0.5)),
        out_shape=(
            jax.ShapeDtypeStruct((rows, width), BF16),
            jax.ShapeDtypeStruct((rows, width), BF16),
            jax.ShapeDtypeStruct((width, width), F32),
        ),
        in_specs=[whole, whole, whole],
        out_specs=(whole, whole, whole),
    )(act, grad_t, weight_sum)


def solution(mesh):
    in_specs = (
        P(("dom", "repl"), None),
        P(("dom", "repl"), None),
        P(),
        P("dom", "repl", None, None, None, None),
        P("dom", "repl", None, None),
        P("dom", "repl", None, None),
        P("dom", "repl", None),
    )
    out_specs = (P(("dom", "repl"), None), P(("dom", "repl"), None), P())
    return jax.shard_map(local, mesh=mesh, in_specs=in_specs, out_specs=out_specs, check_vma=False)
```

```python
import functools

import jax
import jax.numpy as jnp
from jax import lax
from jax.experimental import pallas as pl
from jax.experimental.pallas import tpu as pltpu
from jax.sharding import PartitionSpec as P

F32 = jnp.float32
BF16 = jnp.bfloat16
MESH = pl.DeviceIdType.MESH
Z, YH, CO, YL, X = 4, 2, 2, 2, 4
NDOM, NREP = Z * YH * CO, YL * X
VMEM_LIMIT = 60 << 20


class Names:
    def __init__(self):
        self.count = 0

    def take(self, n=1):
        base = self.count
        self.count += n
        return base


def message_table():
    names = Names()
    table = {}
    gather = ("y0", "y1", "nu0", "nu1", "nd0", "nd1", "fu", "fd", "hd", "hu", "pu", "pd", "qu", "qd")
    reduce = ("f0u", "f0d", "f1u", "f1d", "yu", "yd", "tu", "td", "ou0", "ou1", "od0", "od1", "y0", "y1")
    for h in (0, 1):
        for phase, kinds, siblings in (("A", gather, 8), ("B", reduce, 0), ("D", gather, 0), ("E", reduce, 8)):
            for kind in kinds:
                table[phase, kind, h] = names.take()
            if siblings:
                table[phase, "sib", h] = names.take(siblings)
    for kind in ("rc", "gc"):
        table["W", kind] = names.take(1)
    for kind in ("rz", "ry", "rx", "gx", "gy", "gz"):
        table["W", kind] = names.take(3)
    return table, names.count


def kernel(dims, table, trow_ref, tcol_ref, count_ref, feat_ref, cot_any, w_any, tiles_ref,
           act_ref, grad_ref, wgrad_ref, *scratch):
    rows, width, tile, slots = dims
    half = width // 2
    (tbuf, rbuf, adj, fbuf, gbuf, pacc, eacc, agg, preact,
     bs_far, bs_y0, bs_t, bs_o, bs_y, br_far, br_y0, br_t, br_o, br_y,
     es_far, es_y0, es_t, es_o, es_y, er_far, er_y0, er_t, er_o, er_y, ess, ers,
     wpart, wrc, wzb, wrz, w2, wry, w3, wrx, wfull,
     wanted, links, chain_ref, cot_ref, w_ref, isem,
     tsem, fsem, csem, ssem, rsem) = scratch

    dom = lax.axis_index("dom")
    rep = lax.axis_index("repl")
    co = lax.rem(dom, 2)
    yh = lax.rem(lax.div(dom, 2), 2)
    z = lax.div(dom, 4)
    x = lax.rem(rep, 4)
    yl = lax.div(rep, 4)
    y = yh * 2 + yl

    def turn(v, by):
        return lax.rem(v + by, 4)

    zu, zd, z2 = turn(z, 1), turn(z, 3), turn(z, 2)
    xu, xd, x2 = turn(x, 1), turn(x, 3), turn(x, 2)

    def did(z_, yh_, co_):
        return z_ * 4 + yh_ * 2 + co_

    def at_y(y_):
        return (did(z, lax.div(y_, 2), co), lax.rem(y_, 2) * 4 + x)

    dev_sib = (did(z, yh, 1 - co), rep)
    dev_zu, dev_zd = (did(zu, yh, co), rep), (did(zd, yh, co), rep)
    dev_yp = (did(z, 1 - yh, co), rep)
    dev_xu, dev_xd = (dom, yl * 4 + xu), (dom, yl * 4 + xd)
    dev_yl = (dom, (1 - yl) * 4 + x)
    zpeers = [(did(turn(z, k), yh, co), rep) for k in (1, 2, 3)]
    ypeers = [at_y(turn(y, k)) for k in (1, 2, 3)]
    xpeers = [(dom, yl * 4 + turn(x, k)) for k in (1, 2, 3)]

    pending = []

    def send(src, dst, number, dev, slot=None):
        arrival = number if slot is None else number + slot
        copy = pltpu.make_async_remote_copy(
            src_ref=src, dst_ref=dst, send_sem=ssem.at[len(pending)], recv_sem=rsem.at[arrival],
            device_id=dev, device_id_type=MESH)
        copy.start()
        pending.append(copy)

    def arrived(dst, number, slot=None):
        number = number if slot is None else number + slot
        pltpu.make_async_remote_copy(
            src_ref=dst, dst_ref=dst, send_sem=ssem.at[0], recv_sem=rsem.at[number],
            device_id=dev_sib, device_id_type=MESH).wait_recv()

    def slab(c):
        return pl.ds(pl.multiple_of(c * rows, rows), rows)

    for h in (0, 1):
        pltpu.make_async_copy(
            feat_ref.at[:, h * half:(h + 1) * half], fbuf.at[h, slab(dom)], fsem.at[h]).start()
    for c in range(NDOM):
        pltpu.make_async_copy(tiles_ref.at[c], tbuf.at[c], tsem.at[c]).start()
    barrier = pltpu.get_barrier_semaphore()
    partners = [dev_sib] + zpeers + ypeers + xpeers
    for dev in partners:
        pl.semaphore_signal(barrier, inc=1, device_id=dev, device_id_type=MESH)
    loads = [pltpu.make_async_copy(w_any, w_ref, isem.at[0]), pltpu.make_async_copy(cot_any, cot_ref, isem.at[1])]
    for copy in loads:
        copy.start()
    rbuf[slots] = jnp.zeros((tile, tile), F32)

    place = trow_ref[...] * 2 + tcol_ref[...]
    lane = lax.broadcasted_iota(jnp.int32, (NDOM, 128), 1)
    wanted[...] = lane - slots
    wanted[:, :slots] = place
    target = wanted[...]
    square = (NDOM, NDOM)
    diagonal = lax.broadcasted_iota(jnp.int32, square, 0) == lax.broadcasted_iota(jnp.int32, square, 1)
    live = jnp.sum(jnp.where(diagonal, count_ref[...], 0), axis=1, keepdims=True)
    limit = jnp.minimum(jnp.where(lane < slots, lane, slots), live)
    chain = jnp.full((NDOM, 128), slots, jnp.int32)
    for t in range(slots):
        chain = jnp.where((target == place[:, t:t + 1]) & (t < limit), t, chain)
    links[...] = chain
    pl.semaphore_wait(barrier, len(partners))
    load = pltpu.make_async_copy(links, chain_ref, csem)
    load.start()

    def part_of(n, part):
        return pl.ds(0, n) if part is None else pl.ds(part * (n // 2), n // 2)

    def gather(phase, view, dev_u, dev_d, dev_y, after):
        def push(h, kind, dev, *where):
            block = view(h, *where)
            send(block, block, table[phase, kind, h], dev)

        def wait(h, kind, *where):
            arrived(view(h, *where), table[phase, kind, h])

        def pair(h):
            for part in (0, 1):
                push(h, f"y{part}", dev_y, "me", 1, part)
            after(h, "me", 1)

        def near(h, turn_):
            push(h, f"nu{turn_}", dev_u, "me", 1, turn_)
            push(h, f"nd{1 - turn_}", dev_d, "me", 1, 1 - turn_)

        def far(h):
            wait(h, "nu0", "d", 1, 0)
            push(h, "fu", dev_u, "d", 1, 0)
            wait(h, "nd1", "u", 1, 1)
            push(h, "fd", dev_d, "u", 1, 1)

        def side(h):
            wait(h, "nu1", "d", 1, 1)
            push(h, "hd", dev_y, "d", 1, 1)
            wait(h, "nd0", "u", 1, 0)
            push(h, "hu", dev_y, "u", 1, 0)
            after(h, "d", 1)
            after(h, "u", 1)

        def other(h):
            wait(h, "y0", "me", 0, 0)
            push(h, "pu", dev_u, "me", 0, 0)
            wait(h, "y1", "me", 0, 1)
            push(h, "pd", dev_d, "me", 0, 1)
            after(h, "me", 0)

        def far_other(h):
            wait(h, "pu", "d", 0, 0)
            push(h, "qu", dev_u, "d", 0, 0)
            wait(h, "pd", "u", 0, 1)
            push(h, "qd", dev_d, "u", 0, 1)

        def rest(h):
            wait(h, "hd", "d", 0, 1)
            wait(h, "hu", "u", 0, 0)
            after(h, "d", 0)
            after(h, "u", 0)
            wait(h, "fu", "2", 1, 0)
            wait(h, "fd", "2", 1, 1)
            after(h, "2", 1)
            wait(h, "qu", "2", 0, 0)
            wait(h, "qd", "2", 0, 1)
            after(h, "2", 0)

        return pair, near, far, side, other, far_other, rest

    FAR, UP, DOWN, HERE = 0, 1, 2, 3

    def reduce(phase, n, value, acc, buffers, dev_u, dev_d, dev_y):
        s_far, s_y0, s_t, s_o, s_y, r_far, r_y0, r_t, r_o, r_y = buffers
        a, b = part_of(n, 0), part_of(n, 1)

        def push(src, dst, h, kind, dev):
            send(src, dst, table[phase, kind, h], dev)

        def far(h):
            for q in (0, 1):
                s_far[h, q] = value(h, FAR, q, part_of(n, None)).astype(BF16)
                push(s_far.at[h, q, a], r_far.at[h, q, 0], h, f"f{q}u", dev_u)
                push(s_far.at[h, q, b], r_far.at[h, q, 1], h, f"f{q}d", dev_d)

        def pair_up(h):
            s_y0[h, 0] = value(h, UP, 0, b).astype(BF16)
            push(s_y0.at[h, 0], r_y0.at[h, 0], h, "yu", dev_y)

        def pair_down(h):
            s_y0[h, 1] = value(h, DOWN, 0, a).astype(BF16)
            push(s_y0.at[h, 1], r_y0.at[h, 1], h, "yd", dev_y)

        def other(h):
            above, below = value(h, UP, 0, a), value(h, DOWN, 0, b)
            arrived(r_far.at[h, 0, 0], table[phase, "f0u", h])
            s_t[h, 0] = (above + r_far[h, 0, 0].astype(F32)).astype(BF16)
            push(s_t.at[h, 0], r_t.at[h, 0], h, "tu", dev_u)
            arrived(r_far.at[h, 0, 1], table[phase, "f0d", h])
            s_t[h, 1] = (below + r_far[h, 0, 1].astype(F32)).astype(BF16)
            push(s_t.at[h, 1], r_t.at[h, 1], h, "td", dev_d)

        def own(h):
            for i, (kind, dev, name, one, two) in enumerate(((UP, dev_u, "u", a, b), (DOWN, dev_d, "d", b, a))):
                value_one, value_two = value(h, kind, 1, one), value(h, kind, 1, two)
                arrived(r_far.at[h, 1, i], table[phase, f"f1{name}", h])
                s_o[h, i, one] = (value_one + r_far[h, 1, i].astype(F32)).astype(BF16)
                push(s_o.at[h, i, one], r_o.at[h, i, one], h, f"o{name}0", dev)
                arrived(r_y0.at[h, i], table[phase, f"y{name}", h])
                s_o[h, i, two] = (value_two + r_y0[h, i].astype(F32)).astype(BF16)
                push(s_o.at[h, i, two], r_o.at[h, i, two], h, f"o{name}1", dev)

        def pair(h):
            for i, (name, rows_) in enumerate((("u", a), ("d", b))):
                arrived(r_t.at[h, i], table[phase, f"t{name}", h])
                s_y[h, rows_] = (value(h, HERE, 0, rows_) + r_t[h, i].astype(F32)).astype(BF16)
                push(s_y.at[h, rows_], r_y.at[h, rows_], h, f"y{i}", dev_y)

        def collect(h):
            total = value(h, HERE, 1, part_of(n, None))
            for i, (name, one, two) in enumerate((("u", a, b), ("d", b, a))):
                arrived(r_o.at[h, i, one], table[phase, f"o{name}0", h])
                arrived(r_o.at[h, i, two], table[phase, f"o{name}1", h])
            acc[h, HERE, 1] = total + r_o[h, 0].astype(F32) + r_o[h, 1].astype(F32)

        def end(h):
            arrived(r_y.at[h, a], table[phase, "y0", h])
            arrived(r_y.at[h, b], table[phase, "y1", h])
            return acc[h, HERE, 1] + r_y[h].astype(F32)

        return far, pair_up, pair_down, other, own, pair, collect, end

    a_places = [("me", 1), ("me", 0), ("d", 1), ("u", 1), ("d", 0), ("u", 0), ("2", 1), ("2", 0)]

    def a_slot(place, column, core):
        return did({"me": z, "u": zu, "d": zd, "2": z2}[place], yh if column else 1 - yh, core)

    def a_view(h, place, column, part):
        start = a_slot(place, column, co) * rows + (0 if part is None else part * (rows // 2))
        size = rows if part is None else rows // 2
        return fbuf.at[h, pl.ds(pl.multiple_of(start, size), size)]

    def a_after(h, place, column):
        block = a_view(h, place, column, None)
        send(block, block, table["A", "sib", h] + a_places.index((place, column)), dev_sib)

    a_pair, a_near, a_far, a_side, a_other, a_far_other, a_rest = gather("A", a_view, dev_zu, dev_zd, dev_yp, a_after)

    def a_open(h):
        pltpu.make_async_copy(
            feat_ref.at[:, h * half:(h + 1) * half], fbuf.at[h, slab(dom)], fsem.at[h]).wait()
        a_pair(h)

    def a_end(h):
        for i, (place, column) in enumerate(a_places):
            arrived(fbuf.at[h, slab(a_slot(place, column, 1 - co))], table["A", "sib", h] + i)

    def densify(first, last):
        @pl.loop(first, last)
        def _(c):
            pltpu.make_async_copy(tiles_ref.at[c], tbuf.at[c], tsem.at[c]).wait()
            for t in range(slots):
                rbuf[t] = tbuf[c, t].astype(F32) + rbuf[chain_ref[c, t]]
            for p in range(4 * NREP):
                r, k = p // 2, p % 2
                g, i = r // 2, r % 2
                row = ((g % 4 * 2 + g // 4) * 2 + i) * tile
                lane = pl.multiple_of(c * rows + k * tile, tile)
                adj[row:row + tile, pl.ds(lane, tile)] = rbuf[chain_ref[c, slots + p]].astype(BF16)

    def b_part(h, kind):
        x_ = (x2, xu, xd, x)[kind]

        @pl.loop(0, 2)
        def _(i):
            parity = i * yl + (1 - i) * (1 - yl)
            where = pl.multiple_of((x_ * 2 + parity) * rows, rows)
            pacc[h, kind, i] = jnp.dot(adj[pl.ds(where, rows), :], fbuf[h], preferred_element_type=F32)

    def b_value(h, kind, q, part):
        return pacc[h, kind, q, part]

    b_far, b_pair_up, b_pair_down, b_other, b_own, b_pair, b_collect, b_end = reduce(
        "B", rows, b_value, pacc, (bs_far, bs_y0, bs_t, bs_o, bs_y, br_far, br_y0, br_t, br_o, br_y),
        dev_xu, dev_xd, dev_yl)

    def b_close(h):
        agg[:, h * half:(h + 1) * half] = b_end(h).astype(BF16)

    def d_view(h, place, column, part):
        slot = {"me": x, "u": xu, "d": xd, "2": x2}[place] * 2 + (yl if column else 1 - yl)
        return gbuf.at[h, part_of(half, part), pl.ds(pl.multiple_of(slot * rows, rows), rows)]

    d_pair, d_near, d_far, d_side, d_other, d_far_other, d_rest = gather(
        "D", d_view, dev_xu, dev_xd, dev_yl, lambda h, place, column: None)

    def e_part(h, kind):
        z_ = (z2, zu, zd, z)[kind]

        @pl.loop(0, 2)
        def _(i):
            parity = i * yh + (1 - i) * (1 - yh)
            ess[h, kind, i] = jnp.dot(
                gbuf[h], adj[:, slab(did(z_, parity, 1 - co))], preferred_element_type=F32).astype(BF16)
            eacc[h, kind, i] = jnp.dot(
                gbuf[h], adj[:, slab(did(z_, parity, co))], preferred_element_type=F32)

        for i in (0, 1):
            send(ess.at[h, kind, i], ers.at[h, kind, i], table["E", "sib", h] + kind * 2 + i, dev_sib)

    def e_join(h, kind):
        for i in (0, 1):
            arrived(ers.at[h, kind, i], table["E", "sib", h] + kind * 2 + i)

    def e_value(h, kind, q, part):
        return eacc[h, kind, q, part] + ers[h, kind, q, part].astype(F32)

    e_far, e_pair_up, e_pair_down, e_other, e_own, e_pair, e_collect, e_end = reduce(
        "E", half, e_value, eacc, (es_far, es_y0, es_t, es_o, es_y, er_far, er_y0, er_t, er_o, er_y),
        dev_zu, dev_zd, dev_yp)

    def e_close(h):
        grad_ref[h * half:(h + 1) * half, :] = e_end(h).astype(BF16)

    wc, wz, wy = width // 2, width // 8, width // 32
    wl = width // 4

    def at(i, n):
        return pl.ds(pl.multiple_of(i * n, n), n)

    def w_core():
        send(wpart.at[at(1 - co, wc)], wrc, table["W", "rc"], dev_sib)

    def first_at(y_):
        return pl.ds(pl.multiple_of(co * wc + y_ * wz, wz), wz)

    def row_at(z_):
        return pl.ds(pl.multiple_of(co * wc + y * wz + z_ * wy, wy), wy)

    def w_y():
        arrived(wrc, table["W", "rc"])
        wpart[at(co, wc)] = wpart[at(co, wc)] + wrc[...]
        wzb[...] = wpart[at(co, wc)].astype(BF16)
        for k in (1, 2, 3):
            send(wzb.at[at(turn(y, k), wz)], wrz.at[k - 1], table["W", "ry"] + k - 1, ypeers[k - 1])

    def w_z():
        w2[...] = wpart[first_at(y)]
        for k in range(3):
            arrived(wrz.at[k], table["W", "ry"] + k)
            w2[...] += wrz[k].astype(F32)
        for k in (1, 2, 3):
            send(w2.at[at(turn(z, k), wy)], wry.at[k - 1], table["W", "rz"] + k - 1, zpeers[k - 1])

    def w_x():
        total = w2[at(z, wy)]
        for k in range(3):
            arrived(wry.at[k], table["W", "rz"] + k)
            total = total + wry[k]
        w3[...] = total
        for k in (1, 2, 3):
            send(w3.at[:, at(turn(x, k), wl)], wrx.at[k - 1], table["W", "rx"] + k - 1, xpeers[k - 1])

    def w_gx():
        total = w3[:, at(x, wl)]
        for k in range(3):
            arrived(wrx.at[k], table["W", "rx"] + k)
            total = total + wrx[k]
        wfull[row_at(z), at(x, wl)] = total.astype(BF16)
        block = wfull.at[row_at(z), at(x, wl)]
        for k in range(3):
            send(block, block, table["W", "gx"] + k, xpeers[k])

    def w_gz():
        for k in (1, 2, 3):
            arrived(wfull.at[row_at(z), at(turn(x, 4 - k), wl)], table["W", "gx"] + k - 1)
        block = wfull.at[row_at(z)]
        for k in range(3):
            send(block, block, table["W", "gz"] + k, zpeers[k])

    def w_gy():
        for k in (1, 2, 3):
            arrived(wfull.at[row_at(turn(z, 4 - k))], table["W", "gz"] + k - 1)
        block = wfull.at[first_at(y)]
        for k in range(3):
            send(block, block, table["W", "gy"] + k, ypeers[k])

    def w_gc():
        for k in (1, 2, 3):
            arrived(wfull.at[first_at(turn(y, 4 - k))], table["W", "gy"] + k - 1)
        block = wfull.at[at(co, wc)]
        send(block, block, table["W", "gc"], dev_sib)

    def w_end():
        arrived(wfull.at[at(1 - co, wc)], table["W", "gc"])
        wgrad_ref[...] = wfull[...]

    a_open(0)
    a_near(0, 0)
    a_near(0, 1)
    a_open(1)
    a_near(1, 0)
    load.wait()
    densify(0, 6)
    a_far(0)
    a_other(0)
    a_near(1, 1)
    a_side(0)
    densify(6, 10)
    a_other(1)
    a_far_other(0)
    a_far(1)
    a_side(1)
    densify(10, NDOM)
    a_far_other(1)
    a_rest(0)
    a_end(0)
    b_part(0, FAR)
    b_far(0)
    b_part(0, UP)
    b_pair_up(0)
    a_rest(1)
    b_part(0, DOWN)
    b_pair_down(0)
    a_end(1)
    b_other(0)
    b_part(1, FAR)
    b_far(1)
    b_own(0)
    b_part(1, UP)
    b_pair_up(1)
    b_part(1, DOWN)
    b_pair_down(1)
    b_part(0, HERE)
    b_pair(0)
    b_other(1)
    b_part(1, HERE)
    b_own(1)
    b_collect(0)
    b_pair(1)
    b_close(0)
    for copy in loads:
        copy.wait()
    preact[...] = jnp.dot(agg[:, :half], w_ref[:half, :], preferred_element_type=F32)
    b_collect(1)
    b_close(1)

    pre = preact[...] + jnp.dot(agg[:, half:], w_ref[half:, :], preferred_element_type=F32)
    sig = 1.0 / (1.0 + jnp.exp(-pre))
    act_ref[...] = (pre * sig).astype(BF16)
    grad = (cot_ref[...].astype(F32) * (sig * (1.0 + pre * (1.0 - sig)))).astype(BF16)
    for h in (0, 1):
        gbuf[h, :, pl.ds(pl.multiple_of((x * 2 + yl) * rows, rows), rows)] = lax.dot_general(
            w_ref[h * half:(h + 1) * half, :], grad, (((1,), (1,)), ((), ())),
            preferred_element_type=F32).astype(BF16)
        d_pair(h)
        d_near(h, 0)
        if h == 0:
            d_near(h, 1)
    wpart[...] = lax.dot_general(
        agg[...], grad, (((0,), (0,)), ((), ())), preferred_element_type=F32)
    w_core()

    d_far(0)
    d_other(0)
    d_near(1, 1)
    d_side(0)
    w_y()
    d_other(1)
    d_far_other(0)
    d_far(1)
    d_side(1)
    w_z()
    d_far_other(1)
    d_rest(0)
    e_part(0, FAR)
    e_part(0, UP)
    e_join(0, FAR)
    e_far(0)
    w_x()
    e_part(0, DOWN)
    e_join(0, UP)
    e_pair_up(0)
    d_rest(1)
    e_part(1, FAR)
    e_join(0, DOWN)
    e_pair_down(0)
    e_other(0)
    e_part(1, UP)
    e_join(1, FAR)
    e_far(1)
    w_gx()
    e_own(0)
    e_part(1, DOWN)
    e_join(1, UP)
    e_pair_up(1)
    w_gz()
    e_part(0, HERE)
    e_join(1, DOWN)
    e_pair_down(1)
    e_other(1)
    e_join(0, HERE)
    e_pair(0)
    e_part(1, HERE)
    w_gy()
    e_own(1)
    e_join(1, HERE)
    e_pair(1)
    e_collect(0)
    w_gc()
    e_close(0)
    e_collect(1)
    w_end()
    e_close(1)
    for copy in pending:
        copy.wait_send()


def reduce_scratch(n, m):
    shapes = [
        [(2, 2, n, m), (2, 2, n // 2, m), (2, 2, n // 2, m), (2, 2, n, m), (2, n, m)],
        [(2, 2, 2, n // 2, m), (2, 2, n // 2, m), (2, 2, n // 2, m), (2, 2, n, m), (2, n, m)],
    ]
    return [pltpu.VMEM(shape, BF16) for side in shapes for shape in side]


def finish(scale, act_in, grad_in, weight_in, act_out, grad_out, weight_out,
           act, grad, grad_t, weight, weight_f, sem_in, sem_out):
    moves_in = [
        pltpu.make_async_copy(src, dst, sem_in.at[i])
        for i, (src, dst) in enumerate(((weight_in, weight), (grad_in, grad), (act_in, act)))]
    moves_out = [
        pltpu.make_async_copy(src, dst, sem_out.at[i])
        for i, (src, dst) in enumerate(((weight_f, weight_out), (grad_t, grad_out), (act, act_out)))]
    for move in moves_in:
        move.start()
    moves_in[0].wait()
    weight_f[...] = weight[...].astype(F32) * scale
    moves_out[0].start()
    moves_in[1].wait()
    grad_t[...] = grad[...].T
    moves_out[1].start()
    moves_in[2].wait()
    moves_out[2].start()
    for move in moves_out:
        move.wait()


def local(features, cotangent, weight, tiles, tile_rows, tile_cols, tile_counts):
    rows, width = features.shape
    slots, tile = tiles.shape[3], tiles.shape[-1]
    half = width // 2
    table, count = message_table()
    dims = (rows, width, tile, slots)
    vmem = pltpu.VMEM
    scratch = [
        vmem((NDOM, slots, tile, tile), BF16),
        vmem((slots + 1, tile, tile), F32),
        vmem((NREP * rows, NDOM * rows), BF16),
        vmem((2, NDOM * rows, half), BF16),
        vmem((2, half, NREP * rows), BF16),
        vmem((2, 4, 2, rows, half), F32),
        vmem((2, 4, 2, half, rows), F32),
        vmem((rows, width), BF16),
        vmem((rows, width), F32),
        *reduce_scratch(rows, half),
        *reduce_scratch(half, rows),
        vmem((2, 4, 2, half, rows), BF16),
        vmem((2, 4, 2, half, rows), BF16),
        vmem((width, width), F32),
        vmem((width // 2, width), F32),
        vmem((width // 2, width), BF16),
        vmem((3, width // 8, width), BF16),
        vmem((width // 8, width), F32),
        vmem((3, width // 32, width), F32),
        vmem((width // 32, width), F32),
        vmem((3, width // 32, width // 4), F32),
        vmem((width, width), BF16),
        vmem((NDOM, 128), jnp.int32),
        vmem((NDOM, 128), jnp.int32),
        pltpu.SMEM((NDOM, 128), jnp.int32),
        vmem((rows, width), BF16),
        vmem((width, width), BF16),
        pltpu.SemaphoreType.DMA((2,)),
        pltpu.SemaphoreType.DMA((NDOM,)),
        pltpu.SemaphoreType.DMA((2,)),
        pltpu.SemaphoreType.DMA,
        pltpu.SemaphoreType.DMA((count,)),
        pltpu.SemaphoreType.DMA((count,)),
    ]
    whole = pl.BlockSpec(memory_space=pltpu.VMEM)
    anywhere = pl.BlockSpec(memory_space=pl.ANY)
    act, grad_t, weight_sum = pl.pallas_call(
        functools.partial(kernel, dims, table),
        out_shape=(
            jax.ShapeDtypeStruct((rows, width), BF16),
            jax.ShapeDtypeStruct((width, rows), BF16),
            jax.ShapeDtypeStruct((width, width), BF16),
        ),
        in_specs=[whole, whole, whole, anywhere, anywhere, anywhere, anywhere],
        out_specs=(whole, whole, whole),
        scratch_shapes=scratch,
        compiler_params=pltpu.CompilerParams(
            collective_id=0, has_side_effects=True, vmem_limit_bytes=VMEM_LIMIT),
    )(tile_rows[0, 0], tile_cols[0, 0], tile_counts[0], features, cotangent, weight, tiles[0, 0])
    return pl.pallas_call(
        functools.partial(finish, float(rows * NDOM * NREP) ** (-0.5)),
        out_shape=(
            jax.ShapeDtypeStruct((rows, width), BF16),
            jax.ShapeDtypeStruct((rows, width), BF16),
            jax.ShapeDtypeStruct((width, width), F32),
        ),
        in_specs=[anywhere, anywhere, anywhere],
        out_specs=(anywhere, anywhere, anywhere),
        scratch_shapes=[
            vmem((rows, width), BF16),
            vmem((width, rows), BF16),
            vmem((rows, width), BF16),
            vmem((width, width), BF16),
            vmem((width, width), F32),
            pltpu.SemaphoreType.DMA((3,)),
            pltpu.SemaphoreType.DMA((3,)),
        ],
    )(act, grad_t, weight_sum)


def solution(mesh):
    in_specs = (
        P(("dom", "repl"), None),
        P(("dom", "repl"), None),
        P(),
        P("dom", "repl", None, None, None, None),
        P("dom", "repl", None, None),
        P("dom", "repl", None, None),
        P("dom", "repl", None),
    )
    out_specs = (P(("dom", "repl"), None), P(("dom", "repl"), None), P())
    return jax.shard_map(local, mesh=mesh, in_specs=in_specs, out_specs=out_specs, check_vma=False)
```
